128 devices in a mesh: space: 8 (over z, core), scene: 16 (over x, y).
Axes of the slice: x: 4, y: 4, z: 4, core: 2. Of those that a mesh axis runs over, the one named last changes fastest.
Arguments:
- pixels: bfloat16 [32, 128, 64, 384], P('scene', 'space'), may hold values from -6 to 6
- dw_kernel: bfloat16 [7, 7, 384], replicated, may hold values from -0.875 to 0.875
- dw_bias: float32 [384], replicated, may hold values from -3 to 3
- norm_gain: float32 [384], replicated, may hold values from 0.25 to 1.75
- w_expand: bfloat16 [384, 1536], replicated, may hold values from -0.3125 to 0.3125
- w_reduce: bfloat16 [1536, 384], replicated, may hold values from -0.15625 to 0.15625
- layer_scale: float32 [384], replicated, may hold values from 0.3 to 1
- pixel_slot: int32 [32, 128, 64], P('scene', 'space'), may hold values from 0 to 255
- intersection: int32 [128, 256], P(('space', 'scene')), may hold values from 0 to 8191, as said below
- parcel_pos: int32 [8192], replicated, may hold values from 0 to 8191, as said below
- parcel_embed: bfloat16 [8192, 384], P(('space', 'scene')), may hold values from -6 to 6
- attn_gain: float32 [384], replicated, may hold values from 0.25 to 1.75
- w_qkv: bfloat16 [384, 1152], replicated, may hold values from -0.91855865 to 0.91855865
- w_out: bfloat16 [384, 384], replicated, may hold values from -0.3125 to 0.3125
- w_class: bfloat16 [384, 20], replicated, may hold values from -10.7165176 to 10.7165176
- labels: int32 [8192], P(('space', 'scene')), may hold values from 0 to 19
Outputs:
- features: bfloat16 [32, 128, 64, 384], P('scene', 'space')
- parcel_state: bfloat16 [8192, 384], P(('space', 'scene'))
- loss: float32 [8192], P(('space', 'scene'))
The draws below stay inside these ranges and needn't reach their ends.
Inputs may be any that keep to these rules, and one draw needn't show every extreme that they name: `intersection`: row t lists 256 distinct parcels; each owner (positions o * 64 to o * 64 + 63) holds 1 to 3 of them, and in every tile some owner holds exactly 3. `parcel_pos`: each position occurs once.
All inputs are finite; a program needn't handle non-finite values.
Results may differ from the reference program's by a relative error of at most 0.035.
The reference program's roundings to bfloat16 on the way (of `normed`, `hidden`, `attn_in`, `queries`, `keys`, `values`, `attended` and `class_in`) count: a program that leaves them out, or rounds other values in their place, can miss the bound.
Values may be sent and summed in bfloat16 or wider, within the bound.
A program may use at most 128 MiB of HBM per device.

```python
import math
import jax
import jax.numpy as jnp
from jax import lax

C = 384
HID = 1536
KSZ = 7
SCN_DEV = 2
ROWS_DEV = 16
WIDTH_PX = 64
PAR_DEV = 64
HEADS = 6
HEAD_DIM = 64
CLASSES = 20
TILES = 128
K_TILE = 256
PARCELS = 8192
SCENES = 32
ROWS = 128
N_SCENE = 16


def ownership(key):
    base_key = jax.random.fold_in(key, 7)
    pos_perm = jax.random.permutation(jax.random.fold_in(base_key, 1), PARCELS).astype(jnp.int32)
    inverse = jnp.zeros((PARCELS,), jnp.int32).at[pos_perm].set(jnp.arange(PARCELS, dtype=jnp.int32))

    def one_tile(tile_index):
        tile_key = jax.random.fold_in(base_key, tile_index + 2)
        subkeys = jax.random.split(tile_key, 4)
        owner_order = jax.random.permutation(subkeys[0], TILES).astype(jnp.int32)
        first_load = jax.random.randint(subkeys[1], (TILES // 2,), 1, 4).astype(jnp.int32)
        first_load = first_load.at[0].set(3)
        paired = jnp.stack([first_load, 4 - first_load], axis=1).reshape(-1)
        load_count = jnp.zeros((TILES,), jnp.int32).at[owner_order].set(paired)
        owner_dev = jnp.repeat(jnp.arange(TILES, dtype=jnp.int32), load_count, total_repeat_length=K_TILE)
        starts = jnp.cumsum(load_count) - load_count
        slot_rank = jnp.arange(K_TILE, dtype=jnp.int32) - starts[owner_dev]
        offset = jax.random.randint(subkeys[2], (TILES,), 0, PAR_DEV).astype(jnp.int32)
        local_row = (offset[owner_dev] + slot_rank * (PAR_DEV // 3)) % PAR_DEV
        position = owner_dev * PAR_DEV + local_row
        shuffle = jax.random.permutation(subkeys[3], K_TILE)
        return inverse[position[shuffle]]
    intersection = jax.vmap(one_tile)(jnp.arange(TILES, dtype=jnp.int32))
    return (pos_perm, intersection.astype(jnp.int32))


def draw_intersection(key, part):
    return ownership(key)[1]


def draw_parcel_pos(key, part):
    return ownership(key)[0]


def draw_w_qkv(key, part):
    spread = jax.random.uniform(jax.random.fold_in(key, 11), (C, 3 * C), jnp.float32, -1.7, 1.7) * C ** (-0.5)
    return spread.astype(jnp.bfloat16)


def draw_w_class(key, part):
    spread = jax.random.uniform(jax.random.fold_in(key, 13), (C, CLASSES), jnp.float32, -1.7, 1.7) * (4.0 * C ** (-0.5))
    return spread.astype(jnp.bfloat16)


def place_ends(array, key, least, top_value):
    place = [jax.random.randint(jax.random.fold_in(key, axis), (), 0, length) for axis, length in enumerate(array.shape)]
    longest = array.shape.index(max(array.shape))
    neighbour = place[:longest] + [(place[longest] + 1) % array.shape[longest]] + place[longest + 1:]
    return array.at[tuple(place)].set(least).at[tuple(neighbour)].set(top_value)


def levels(stream_key, extent, cuts, least, high):
    factor_of = 1.0
    for dim, parts in cuts:
        draws = jax.random.uniform(jax.random.fold_in(jax.random.fold_in(stream_key, 6), dim), (parts,), jnp.float32, least / len(cuts), high / len(cuts))
        factor_of = factor_of * jnp.repeat(jnp.exp(draws), extent[dim] // parts).reshape((-1,) + (1,) * (len(extent) - 1 - dim))
    return factor_of


def centred(own_key, dims, width, bound, shards=(), kind=jnp.bfloat16):
    drawn = jax.random.normal(own_key, dims, jnp.float32) * width
    if len(shards) > 0:
        drawn = levels(own_key, dims, shards, -0.22, 0.18) * drawn
    return jnp.clip(drawn, min=-bound, max=bound).astype(kind)


def setup_inputs(seed: int = 0) -> dict:
    seeds = jax.random.split(jax.random.key(seed), 17)
    return {
        "pixels": centred(seeds[0], (SCENES, ROWS, WIDTH_PX, C), 1.0, 6.0, ((0, 16), (1, 8))),
        "dw_kernel": centred(seeds[1], (KSZ, KSZ, C), (KSZ * KSZ) ** -0.5, 0.875),
        "dw_bias": centred(seeds[2], (C,), 0.5, 3.0, (), jnp.float32),
        "norm_gain": jnp.clip(1.0 + 0.15 * jax.random.normal(seeds[3], (C,), jnp.float32), 0.25, 1.75),
        "w_expand": centred(seeds[4], (C, HID), C ** -0.5, 0.3125),
        "w_reduce": centred(seeds[5], (HID, C), HID ** -0.5, 0.15625),
        "layer_scale": jnp.clip(jnp.exp(jax.random.uniform(seeds[6], (C,), jnp.float32, math.log(0.3), math.log(1.0))), 0.3, 1.0),
        "pixel_slot": place_ends(jax.random.randint(seeds[7], (SCENES, ROWS, WIDTH_PX), 0, K_TILE), jax.random.fold_in(seeds[7], 1), 0, K_TILE - 1).astype(jnp.int32),
        "intersection": draw_intersection(jax.random.fold_in(seeds[16], 71), 0),
        "parcel_pos": draw_parcel_pos(jax.random.fold_in(seeds[16], 71), 0),
        "parcel_embed": centred(seeds[10], (PARCELS, C), 1.0, 6.0, ((0, 128),)),
        "attn_gain": jnp.clip(1.0 + 0.15 * jax.random.normal(seeds[11], (C,), jnp.float32), 0.25, 1.75),
        "w_qkv": draw_w_qkv(jax.random.fold_in(seeds[16], 71), 0),
        "w_out": centred(seeds[13], (C, C), C ** -0.5, 0.3125),
        "w_class": draw_w_class(jax.random.fold_in(seeds[16], 71), 0),
        "labels": place_ends(jax.random.randint(seeds[15], (PARCELS,), 0, CLASSES), jax.random.fold_in(seeds[15], 1), 0, CLASSES - 1).astype(jnp.int32),
    }


epsilon = 1e-06

def layer_norm(values):
    average = lax.optimization_barrier(jnp.mean(values, axis=-1, keepdims=True))
    centered = values - average
    return centered * lax.rsqrt(lax.optimization_barrier(jnp.mean(centered * centered, axis=-1, keepdims=True)) + epsilon)

def convnext_block(padded, center, dw_kernel, dw_bias, norm_gain, w_expand, w_reduce, layer_scale):
    height = center.shape[1]
    breadth = center.shape[2]
    kernel_f32 = dw_kernel.astype(jnp.float32)
    spatial = jnp.zeros(center.shape, jnp.float32)
    for row_off in range(dw_kernel.shape[0]):
        for col_off in range(dw_kernel.shape[1]):
            window = padded[:, row_off:row_off + height, col_off:col_off + breadth, :]
            spatial = spatial + window.astype(jnp.float32) * kernel_f32[row_off, col_off]
    spatial = spatial + dw_bias
    normed = (layer_norm(spatial) * norm_gain).astype(jnp.bfloat16)
    channels = center.shape[-1]
    flattened = normed.reshape(-1, channels)
    hidden = jax.nn.gelu(jnp.dot(flattened, w_expand, preferred_element_type=jnp.float32), approximate=False).astype(jnp.bfloat16)
    branch = jnp.dot(hidden, w_reduce, preferred_element_type=jnp.float32).reshape(center.shape)
    return (center.astype(jnp.float32) + layer_scale * branch).astype(jnp.bfloat16)

def reference(pixels, dw_kernel, dw_bias, norm_gain, w_expand, w_reduce, layer_scale, pixel_slot, intersection, parcel_pos, parcel_embed, attn_gain, w_qkv, w_out, w_class, labels):

    def one_scene(scene_map):
        padded = jnp.pad(scene_map, ((3, 3), (3, 3), (0, 0)))[None]
        return convnext_block(padded, scene_map[None], dw_kernel, dw_bias, norm_gain, w_expand, w_reduce, layer_scale)[0]
    features = lax.map(one_scene, pixels)
    anchor = jnp.zeros((), jnp.int32)

    def pool_tile(tile_index, running):
        parcel_table, totals = running
        tile_index = jnp.asarray(tile_index).astype(jnp.int32)
        space_index = tile_index // N_SCENE
        scene_index = tile_index % N_SCENE
        first_scene = (scene_index * SCN_DEV).astype(jnp.int32)
        first_row = (space_index * ROWS_DEV).astype(jnp.int32)
        tile_block = lax.dynamic_slice(features, (first_scene, first_row, anchor, anchor), (SCN_DEV, ROWS_DEV, WIDTH_PX, C))
        slot_block = lax.dynamic_slice(pixel_slot, (first_scene, first_row, anchor), (SCN_DEV, ROWS_DEV, WIDTH_PX)).reshape(-1)
        membership = (jnp.arange(K_TILE, dtype=jnp.int32)[:, None] == slot_block[None, :]).astype(jnp.bfloat16)
        slot_sums = jnp.dot(membership, tile_block.reshape(-1, C), preferred_element_type=jnp.float32)
        slot_counts = lax.optimization_barrier(jnp.sum(membership.astype(jnp.float32), axis=1))
        parcels_here = lax.dynamic_index_in_dim(intersection, tile_index, 0, keepdims=False)
        positions = jnp.take(parcel_pos, parcels_here)
        return (parcel_table.at[positions].add(slot_sums), totals.at[positions].add(slot_counts))
    parcel_table, totals = lax.fori_loop(0, TILES, pool_tile, (jnp.zeros((PARCELS, C), jnp.float32), jnp.zeros((PARCELS,), jnp.float32)))
    tokens = parcel_table / jnp.maximum(totals, 1.0)[:, None] + parcel_embed.astype(jnp.float32)
    attn_in = (layer_norm(tokens) * attn_gain).astype(jnp.bfloat16)
    projected = jnp.dot(attn_in, w_qkv, preferred_element_type=jnp.float32)
    queries = lax.optimization_barrier((projected[:, :C] * HEAD_DIM ** (-0.5)).astype(jnp.bfloat16))
    key_value = lax.optimization_barrier(projected[:, C:].astype(jnp.bfloat16))
    keys = key_value[:, :C].astype(jnp.float32).reshape(PARCELS, HEADS, HEAD_DIM)
    values = key_value[:, C:].astype(jnp.float32).reshape(PARCELS, HEADS, HEAD_DIM)

    def attend(query_block):
        query_f32 = query_block.astype(jnp.float32)
        scores = jnp.einsum('qhd,khd->hqk', query_f32, keys)
        top_score = lax.optimization_barrier(jnp.max(scores, axis=-1, keepdims=True))
        weights = jnp.exp(scores - top_score)
        row_total = lax.optimization_barrier(jnp.sum(weights, axis=-1))
        rounded = lax.optimization_barrier(weights.astype(jnp.bfloat16)).astype(jnp.float32)
        mixed_heads = jnp.einsum('hqk,khd->qhd', rounded, values)
        return mixed_heads / jnp.transpose(row_total)[:, :, None]
    attended = lax.map(attend, queries.reshape(TILES, PAR_DEV, HEADS, HEAD_DIM))
    attended = attended.reshape(PARCELS, C).astype(jnp.bfloat16)
    parcel_out = tokens + jnp.dot(attended, w_out, preferred_element_type=jnp.float32)
    class_in = layer_norm(parcel_out).astype(jnp.bfloat16)
    logits = jnp.dot(class_in, w_class, preferred_element_type=jnp.float32)
    top_logit = lax.optimization_barrier(jnp.max(logits, axis=-1, keepdims=True))
    log_total = top_logit[:, 0] + jnp.log(lax.optimization_barrier(jnp.sum(jnp.exp(logits - top_logit), axis=-1)))
    picked = lax.optimization_barrier(jnp.sum(jnp.where(jnp.arange(CLASSES, dtype=jnp.int32)[None, :] == labels[:, None], logits, 0.0), axis=-1))
    return (features, parcel_out.astype(jnp.bfloat16), log_total - picked)
```

```python
import jax
import jax.numpy as jnp
from jax import lax
from jax.experimental import pallas as pl
from jax.experimental.pallas import tpu as pltpu
from jax.sharding import PartitionSpec as P

EPS = 1e-06
N_SPACE = 8
N_SCENE = 16
DEVS = N_SPACE * N_SCENE
PAR = 64
CAP = 3
MSG = 16
F32 = jnp.float32
BF16 = jnp.bfloat16
MESH = pl.DeviceIdType.MESH


def mm(a, b):
    return jnp.dot(a, b, preferred_element_type=F32)


def mm_t(a, b):
    return lax.dot_general(a, b, (((0,), (0,)), ((), ())), preferred_element_type=F32)


def mm_nt(a, b):
    return lax.dot_general(a, b, (((1,), (1,)), ((), ())), preferred_element_type=F32)


def onehot(cond):
    return jnp.where(cond, 1.0, 0.0).astype(BF16)


def iota(shape, dim):
    return lax.broadcasted_iota(jnp.int32, shape, dim)


def layer_norm(x):
    centered = x - jnp.mean(x, axis=-1, keepdims=True)
    return centered * lax.rsqrt(jnp.mean(centered * centered, axis=-1, keepdims=True) + EPS)


def gelu(x):
    return 0.5 * x * (1.0 + lax.erf(x * 0.7071067811865476))


def block_kernel(pix_hbm, up_ref, dn_ref, k_ref, bias_ref, gain_ref, w1_ref, w2_ref, ls_ref, slot_ref, pos_ref,
                 feat_ref, send_ref, xs, kb, vs, sp, ssum, scnt, shm, stg, sem):
    i = pl.program_id(0)

    @pl.when(i == 0)
    def _():
        cps = [pltpu.make_async_copy(pix_hbm.at[s], xs.at[s, pl.ds(3, 16)], sem.at[s]) for s in range(2)]
        for cp in cps:
            cp.start()
        for s in range(2):
            xs[s, 0:3] = up_ref[s]
            xs[s, 19:22] = dn_ref[s]
        for a in range(7):
            k32 = k_ref[a].astype(F32)
            for b in range(7):
                kb[a * 7 + b] = jnp.broadcast_to(k32[b:b + 1, :], (16, 384)).astype(BF16)
        j = iota((64, 448), 1)
        shm[...] = onehot(j % 64 == iota((64, 448), 0) + j // 64 - 3)
        ssum[...] = jnp.zeros_like(ssum)
        scnt[...] = jnp.zeros_like(scnt)
        for cp in cps:
            cp.wait()

    s = i // 4
    r0 = (i % 4) * 4
    for r in range(4):
        for c in range(3):
            cs = pl.ds(c * 128, 128)
            acc = [None] * 7
            for a in range(7):
                x = xs[s, r0 + r + a, :, :, cs]
                for b in range(7):
                    p = x * kb[a * 7 + b, :, cs][None]
                    acc[b] = p if acc[b] is None else acc[b] + p
            for b in range(7):
                vs[b, :, :, cs] = acc[b]
        sp[pl.ds(r * 64, 64), :] = mm(shm[...], vs[...].reshape(448, 384)) + bias_ref[...][None, :]
    nrm = (layer_norm(sp[...]) * gain_ref[...][None, :]).astype(BF16)
    out = None
    for h in range(6):
        hs = pl.ds(h * 256, 256)
        d = mm(gelu(mm(nrm, w1_ref[:, hs])).astype(BF16), w2_ref[hs, :])
        out = d if out is None else out + d
    cen = xs[s, pl.ds(r0 + 3, 4)].reshape(256, 384)
    f = (cen.astype(F32) + ls_ref[...][None, :] * out).astype(BF16)
    feat_ref[...] = f.reshape(feat_ref.shape)
    m = onehot(iota((256, 256), 0) == slot_ref[...].reshape(1, 256))
    ssum[...] += mm(m, f)
    scnt[...] += mm(m, jnp.ones((256, 128), BF16))

    @pl.when(i == pl.num_programs(0) - 1)
    def _():
        pos = pos_ref[...]
        lane = iota((256, 128), 1)
        mine = pos // PAR == lane
        rank = mm(onehot(iota((256, 256), 1) < iota((256, 256), 0)), onehot(mine))
        cnt = scnt[...]
        high = jnp.floor(cnt * (1.0 / 64.0))
        meta = jnp.where(lane == 64, high, jnp.where(lane == 65, cnt - 64.0 * high, jnp.where(lane == pos % PAR, 1.0, 0.0)))
        body = jnp.concatenate([ssum[...], meta], axis=1).astype(BF16)
        for j in range(CAP):
            placed = mm_t(onehot(mine & (rank == j)), body)
            for c in range(4):
                stg[pl.ds(4 * j + c, 128, stride=MSG), :] = placed[:, c * 128:(c + 1) * 128]
        for q in range(4 * CAP, MSG):
            stg[pl.ds(q, 128, stride=MSG), :] = jnp.zeros((128, 128), F32)
        send_ref[...] = stg[...].reshape(128, MSG, 128).astype(BF16)


def block(pixels, up, dn, dw_kernel, bias, gain, w1, w2, ls, slot, pos):
    full = lambda a: pl.BlockSpec(a.shape, lambda i, n=a.ndim: (0,) * n)
    args = (
        pixels.reshape(2, 16, 4, 16, 384), up.reshape(2, 3, 4, 16, 384), dn.reshape(2, 3, 4, 16, 384),
        dw_kernel, bias, gain, w1, w2, ls, slot.reshape(8, 1, 256), pos.reshape(256, 1),
    )
    specs = [pl.BlockSpec(memory_space=pl.ANY)] + [full(a) for a in args[1:9]]
    specs += [pl.BlockSpec((1, 1, 256), lambda i: (i, 0, 0)), full(args[10])]
    feat, send = pl.pallas_call(
        block_kernel,
        grid=(8,),
        out_shape=(jax.ShapeDtypeStruct((2, 16, 4, 16, 384), BF16), jax.ShapeDtypeStruct((128, MSG, 128), BF16)),
        in_specs=specs,
        out_specs=(
            pl.BlockSpec((1, 4, 4, 16, 384), lambda i: (i // 4, i % 4, 0, 0, 0)),
            pl.BlockSpec((128, MSG, 128), lambda i: (0, 0, 0)),
        ),
        scratch_shapes=[
            pltpu.VMEM((2, 22, 4, 16, 384), BF16),
            pltpu.VMEM((49, 16, 384), BF16),
            pltpu.VMEM((7, 4, 16, 384), BF16),
            pltpu.VMEM((256, 384), F32),
            pltpu.VMEM((256, 384), F32),
            pltpu.VMEM((256, 128), F32),
            pltpu.VMEM((64, 448), BF16),
            pltpu.VMEM((2048, 128), F32),
            pltpu.SemaphoreType.DMA((2,)),
        ],
        compiler_params=pltpu.CompilerParams(vmem_limit_bytes=40 << 20),
        name="block",
    )(*args)
    return feat.reshape(2, 16, 64, 384), send


def parcel_kernel(send, embed_ref, gain_ref, wqkv_ref, wout_ref, wcls_ref, lab_ref, state_ref, loss_ref,
                  recv, x32, ain, aq, ak, qb, kb, vb, outb, inb, ssem, rsem):
    sp = lax.axis_index("space")
    sc = lax.axis_index("scene")
    me = sp * N_SCENE + sc

    barrier = pltpu.get_barrier_semaphore()

    def greet(k, carry):
        o = lax.rem(me + k, DEVS)
        pl.semaphore_signal(barrier, inc=1, device_id=(o // N_SCENE, o % N_SCENE), device_id_type=MESH)
        return carry

    lax.fori_loop(1, DEVS, greet, 0)
    pl.semaphore_wait(barrier, DEVS - 1)

    def push(src, dst, n, dev):
        return pltpu.make_async_remote_copy(
            src_ref=src, dst_ref=dst, send_sem=ssem.at[n], recv_sem=rsem.at[n], device_id=dev, device_id_type=MESH
        )

    here = (sp, sc)

    def scatter(k, carry):
        o = lax.rem(me + k, DEVS)
        push(send.at[o], recv.at[me], 0, (o // N_SCENE, o % N_SCENE)).start()
        return carry

    lax.fori_loop(1, DEVS, scatter, 0)
    recv[me] = send[me]
    push(send.at[pl.ds(0, DEVS - 1)], recv.at[pl.ds(0, DEVS - 1)], 0, here).wait()

    x32[...] = recv[...].reshape(DEVS * MSG, 128).astype(F32)
    row = lambda q: x32[pl.ds(q, DEVS, stride=MSG), :].astype(BF16)
    picks = jnp.concatenate([row(4 * j + 3) for j in range(CAP)], axis=0)
    body = jnp.concatenate(
        [jnp.concatenate([row(4 * j + c) for c in range(4)], axis=1) for j in range(CAP)], axis=0
    )
    pooled = mm_t(picks, body)[:PAR]
    lane = iota((PAR, 128), 1)
    tail = pooled[:, 384:]
    count = jnp.sum(jnp.where(lane == 64, 64.0 * tail, jnp.where(lane == 65, tail, 0.0)), axis=-1, keepdims=True)
    tokens = pooled[:, :384] / jnp.maximum(count, 1.0) + embed_ref[...].astype(F32)
    attn_in = (layer_norm(tokens) * gain_ref[...][None, :]).astype(BF16)
    ain[...] = attn_in
    aq[sp] = attn_in
    ak[sc] = attn_in

    def send_q(k, carry):
        push(ain, aq.at[sp], 1, (lax.rem(sp + k, N_SPACE), sc)).start()
        return carry

    def send_k(k, carry):
        push(ain, ak.at[sc], 2, (sp, lax.rem(sc + k, N_SCENE))).start()
        return carry

    lax.fori_loop(1, N_SPACE, send_q, 0)
    lax.fori_loop(1, N_SCENE, send_k, 0)
    push(aq.at[pl.ds(0, N_SPACE - 1)], aq.at[pl.ds(0, N_SPACE - 1)], 1, here).wait()
    qb[...] = (mm(aq[...].reshape(N_SPACE * PAR, 384), wqkv_ref[:, :384]) * 0.125).astype(BF16)
    push(ak.at[pl.ds(0, N_SCENE - 1)], ak.at[pl.ds(0, N_SCENE - 1)], 2, here).wait()
    keys_in = ak[...].reshape(N_SCENE * PAR, 384)
    kb[...] = mm(keys_in, wqkv_ref[:, 384:768]).astype(BF16)
    values = mm(keys_in, wqkv_ref[:, 768:]).astype(BF16)
    for p in range(3):
        vb[:, p * 256:p * 256 + 128] = values[:, p * 128:(p + 1) * 128]
        vb[:, p * 256 + 128:(p + 1) * 256] = jnp.ones((N_SCENE * PAR, 128), BF16)

    rows = N_SPACE * PAR // 2
    lanes = iota((rows, 128), 1)
    for t in range(2):
        ts = pl.ds(t * rows, rows)
        stats = jnp.zeros((rows, 128), F32)
        for p in range(3):
            ps = pl.ds(p * 128, 128)
            q = qb[ts, ps]
            mixed = None
            for u in range(2):
                h = 2 * p + u
                scores = mm_nt(jnp.where((lanes >= 64) == (u == 1), q, jnp.zeros_like(q)), kb[:, ps])
                top = jnp.max(scores, axis=-1, keepdims=True)
                weights = jnp.exp(scores - top).astype(BF16)
                both = mm(weights, vb[:, p * 256:(p + 1) * 256])
                total = both[:, 128:]
                part = both[:, :128] / total
                mixed = part if u == 0 else jnp.where(lanes < 64, mixed, part)
                lse = top + jnp.log(total)
                s0 = lse.astype(BF16).astype(F32)
                s1 = (lse - s0).astype(BF16).astype(F32)
                s2 = lse - s0 - s1
                stats = jnp.where(lanes == h, s0, jnp.where(lanes == 8 + h, s1, jnp.where(lanes == 16 + h, s2, stats)))
            outb[pl.ds(t * 4, 4), :, ps] = mixed.astype(BF16).reshape(4, PAR, 128)
        outb[pl.ds(t * 4, 4), :, 384:] = stats.astype(BF16).reshape(4, PAR, 128)

    def send_o(k, carry):
        o = lax.rem(sp + k, N_SPACE)
        push(outb.at[o], inb.at[sp], 3, (o, sc)).start()
        return carry

    lax.fori_loop(1, N_SPACE, send_o, 0)
    inb[sp] = outb[sp]
    push(outb.at[pl.ds(0, N_SPACE - 1)], inb.at[pl.ds(0, N_SPACE - 1)], 3, here).wait()

    spread = onehot((iota((128, 384), 0) % 8 == iota((128, 384), 1) // 64) & (iota((128, 384), 0) < 24))
    lse = mm(inb[:, :, 384:].reshape(N_SPACE * PAR, 128), spread).reshape(N_SPACE, PAR, 384)
    share = jnp.exp(lse - jnp.max(lse, axis=0, keepdims=True))
    attended = jnp.sum(share * inb[:, :, :384].astype(F32), axis=0) / jnp.sum(share, axis=0)
    state = tokens + mm(attended.astype(BF16), wout_ref[...])
    state_ref[...] = state.astype(BF16)
    class_in = layer_norm(state).astype(BF16)
    logits = lax.dot_general(wcls_ref[...], class_in, (((0,), (1,)), ((), ())), preferred_element_type=F32)
    peak = jnp.max(logits, axis=0, keepdims=True)
    log_total = peak + jnp.log(jnp.sum(jnp.exp(logits - peak), axis=0, keepdims=True))
    picked = jnp.sum(jnp.where(iota(logits.shape, 0) == lab_ref[...], logits, 0.0), axis=0, keepdims=True)
    loss_ref[...] = log_total - picked


def parcels(send, embed, gain, wqkv, wout, wcls, labels):
    vmem = pl.BlockSpec(memory_space=pltpu.VMEM)
    state, loss = pl.pallas_call(
        parcel_kernel,
        out_shape=(jax.ShapeDtypeStruct((PAR, 384), BF16), jax.ShapeDtypeStruct((1, PAR), F32)),
        in_specs=[vmem] * 7,
        out_specs=(vmem, vmem),
        scratch_shapes=[
            pltpu.VMEM((DEVS, MSG, 128), BF16),
            pltpu.VMEM((DEVS * MSG, 128), F32),
            pltpu.VMEM((PAR, 384), BF16),
            pltpu.VMEM((N_SPACE, PAR, 384), BF16),
            pltpu.VMEM((N_SCENE, PAR, 384), BF16),
            pltpu.VMEM((N_SPACE * PAR, 384), BF16),
            pltpu.VMEM((N_SCENE * PAR, 384), BF16),
            pltpu.VMEM((N_SCENE * PAR, 768), BF16),
            pltpu.VMEM((N_SPACE, PAR, 512), BF16),
            pltpu.VMEM((N_SPACE, PAR, 512), BF16),
            pltpu.SemaphoreType.DMA((4,)),
            pltpu.SemaphoreType.DMA((4,)),
        ],
        compiler_params=pltpu.CompilerParams(vmem_limit_bytes=40 << 20, collective_id=0, has_side_effects=True),
        name="parcels",
    )(send, embed, gain, wqkv, wout, wcls, labels.reshape(1, PAR))
    return state, loss.reshape(PAR)


def local(pixels, dw_kernel, dw_bias, norm_gain, w_expand, w_reduce, layer_scale, pixel_slot, intersection,
          parcel_pos, parcel_embed, attn_gain, w_qkv, w_out, w_class, labels):
    count = lax.axis_size("space")
    ahead = [(i, i + 1) for i in range(count - 1)]
    up = lax.ppermute(pixels[:, 13:], "space", ahead)
    dn = lax.ppermute(pixels[:, :3], "space", [(j, i) for i, j in ahead])
    positions = jnp.take(parcel_pos, intersection[0])
    features, send = block(
        pixels, up, dn, dw_kernel, dw_bias, norm_gain, w_expand, w_reduce, layer_scale, pixel_slot, positions
    )
    state, loss = parcels(send, parcel_embed, attn_gain, w_qkv, w_out, w_class, labels)
    return features, state, loss


def solution(mesh):
    in_specs = (
        P("scene", "space", None, None), P(), P(), P(), P(), P(), P(), P("scene", "space", None),
        P(("space", "scene"), None), P(), P(("space", "scene"), None), P(), P(), P(), P(), P(("space", "scene")),
    )
    out_specs = (P("scene", "space", None, None), P(("space", "scene"), None), P(("space", "scene")))
    return jax.shard_map(local, mesh=mesh, in_specs=in_specs, out_specs=out_specs, check_vma=False)
```

```python
import jax
import jax.numpy as jnp
from jax import lax
from jax.experimental import pallas as pl
from jax.experimental.pallas import tpu as pltpu
from jax.sharding import PartitionSpec as P

EPS = 1e-06
N_SPACE = 8
N_SCENE = 16
DEVS = N_SPACE * N_SCENE
PAR = 64
CAP = 3
MSG = 16
F32 = jnp.float32
BF16 = jnp.bfloat16
MESH = pl.DeviceIdType.MESH


def mm(a, b):
    return jnp.dot(a, b, preferred_element_type=F32)


def mm_t(a, b):
    return lax.dot_general(a, b, (((0,), (0,)), ((), ())), preferred_element_type=F32)


def mm_nt(a, b):
    return lax.dot_general(a, b, (((1,), (1,)), ((), ())), preferred_element_type=F32)


def onehot(cond):
    return jnp.where(cond, 1.0, 0.0).astype(BF16)


def iota(shape, dim):
    return lax.broadcasted_iota(jnp.int32, shape, dim)


def layer_norm(x):
    centered = x - jnp.mean(x, axis=-1, keepdims=True)
    return centered * lax.rsqrt(jnp.mean(centered * centered, axis=-1, keepdims=True) + EPS)


def gelu(x):
    return 0.5 * x * (1.0 + lax.erf(x * 0.7071067811865476))


def fused_kernel(pix_hbm, w1_hbm, w2_hbm, wqkv_hbm, wout_hbm, embed_hbm, k_ref, bias_ref, gain_ref, ls_ref, slot_ref,
                 inter_ref, ppos_ref, again_ref, wcls_ref, lab_ref, feat_hbm, state_ref, loss_ref,
                 xs, taps, vs, sp32, nb, fb, ssum, scnt, shm, w1, w2, wqkv, wout, embed, send, recv, x32, ain, aq, ak,
                 qb, kb, vb, outb, inb, lsem, fsem, ssem, rsem):
    sp = lax.axis_index("space")
    sc = lax.axis_index("scene")
    me = sp * N_SCENE + sc
    here = (sp, sc)

    loads = [pltpu.make_async_copy(pix_hbm.at[s], xs.at[s, pl.ds(3, 16)], lsem.at[s]) for s in range(2)]
    pairs = ((w1_hbm, w1), (w2_hbm, w2), (wqkv_hbm, wqkv), (wout_hbm, wout), (embed_hbm, embed))
    loads += [pltpu.make_async_copy(a, b, lsem.at[2 + n]) for n, (a, b) in enumerate(pairs)]
    for cp in loads:
        cp.start()

    barrier = pltpu.get_barrier_semaphore()

    def greet(k, carry):
        o = lax.rem(me + k, DEVS)
        pl.semaphore_signal(barrier, inc=1, device_id=(o // N_SCENE, o % N_SCENE), device_id_type=MESH)
        return carry

    lax.fori_loop(1, DEVS, greet, 0)

    def push(src, dst, n, dev):
        return pltpu.make_async_remote_copy(
            src_ref=src, dst_ref=dst, send_sem=ssem.at[n], recv_sem=rsem.at[n], device_id=dev, device_id_type=MESH
        )

    to_prev = push(xs.at[:, pl.ds(3, 3)], xs.at[:, pl.ds(19, 3)], 4, (lax.rem(sp + N_SPACE - 1, N_SPACE), sc))
    to_next = push(xs.at[:, pl.ds(16, 3)], xs.at[:, pl.ds(0, 3)], 5, (lax.rem(sp + 1, N_SPACE), sc))
    first, last = sp == 0, sp == N_SPACE - 1

    @pl.when(first)
    def _():
        xs[:, 0:3] = jnp.zeros((2, 3, 4, 16, 384), BF16)

    @pl.when(last)
    def _():
        xs[:, 19:22] = jnp.zeros((2, 3, 4, 16, 384), BF16)

    for a in range(7):
        k32 = k_ref[a].astype(F32)
        for b in range(7):
            taps[a * 7 + b] = jnp.broadcast_to(k32[b:b + 1, :], (16, 384)).astype(BF16)
    j = iota((64, 448), 1)
    shm[...] = onehot(j % 64 == iota((64, 448), 0) + j // 64 - 3)
    ssum[...] = jnp.zeros_like(ssum)
    scnt[...] = jnp.zeros_like(scnt)

    def place(k):
        inner = k < 4
        s = lax.rem(k, 4) // 2
        r0 = jnp.where(inner, 4 + 4 * lax.rem(k, 2), 12 * lax.rem(k, 2))
        return s, r0

    def conv(k):
        s, r0 = place(k)
        slot = lax.rem(k, 2)

        def piece(r, c):
            cs = pl.ds(c * 128, 128)
            acc = [None] * 7
            for a in range(7):
                x = xs[s, r0 + r + a, :, :, cs]
                for b in range(7):
                    p = x * taps[a * 7 + b, :, cs][None]
                    acc[b] = p if acc[b] is None else acc[b] + p
            for b in range(7):
                vs[r, b, :, :, cs] = acc[b]

        def row(r):
            sp32[pl.ds(r * 64, 64), :] = mm(shm[...], vs[r].reshape(448, 384)) + bias_ref[...][None, :]

        def norm():
            nb[slot] = (layer_norm(sp32[...]) * gain_ref[...][None, :]).astype(BF16)

        steps = []
        for r in range(4):
            steps += [lambda r=r, c=c: piece(r, c) for c in range(3)]
            steps.append(lambda r=r: row(r))
        return steps + [norm]

    def mlp(k):
        s, r0 = place(k)
        box = {}

        def part(h):
            hs = pl.ds(h * 256, 256)
            d = mm(gelu(mm(nb[lax.rem(k, 2)], w1[:, hs])).astype(BF16), w2[hs, :])
            box["out"] = d if h == 0 else box["out"] + d

        def finish():
            cen = xs[s, pl.ds(r0 + 3, 4)].reshape(256, 384)
            f = (cen.astype(F32) + ls_ref[...][None, :] * box["out"]).astype(BF16)
            fb[k] = f.reshape(4, 4, 16, 384)
            save(k).start()
            slots = jnp.concatenate([slot_ref[s, pl.ds(r0 + r, 1), :] for r in range(4)], axis=1)
            m = onehot(iota((256, 256), 0) == slots)
            ssum[...] += mm(m, f)
            scnt[...] += mm(m, jnp.ones((256, 128), BF16))

        return [lambda h=h: part(h) for h in range(6)] + [finish]

    def save(k):
        s, r0 = place(k)
        return pltpu.make_async_copy(fb.at[k], feat_hbm.at[s, pl.ds(r0, 4)], fsem.at[k])

    def run(*lists):
        total = max(len(x) for x in lists)
        done = [0] * len(lists)
        for t in range(total):
            for n, x in enumerate(lists):
                while done[n] < len(x) and done[n] * total < (t + 1) * len(x):
                    x[done[n]]()
                    done[n] += 1

    loads[0].wait()
    loads[1].wait()
    run(conv(0))
    loads[2].wait()
    loads[3].wait()

    def stage(k, carry):
        @pl.when(k == 1)
        def _():
            pl.semaphore_wait(barrier, DEVS - 1)

            @pl.when(jnp.logical_not(first))
            def _():
                to_prev.start()

            @pl.when(jnp.logical_not(last))
            def _():
                to_next.start()

        @pl.when(k == 3)
        def _():
            @pl.when(jnp.logical_not(first))
            def _():
                to_prev.wait_send()
                to_next.wait_recv()

            @pl.when(jnp.logical_not(last))
            def _():
                to_next.wait_send()
                to_prev.wait_recv()

        run(mlp(k), conv(k + 1))
        return carry

    lax.fori_loop(0, 7, stage, 0)
    run(mlp(7))

    inter = inter_ref[...]
    hot = onehot(iota((64, 256), 0) == inter // 128)
    low = iota((128, 256), 0) == inter % 128
    table = ppos_ref[...]
    pick = lambda t: jnp.sum(jnp.where(low, mm_t(t.astype(F32).astype(BF16), hot), 0.0), axis=0, keepdims=True)
    owner = pick(table // PAR)
    inrow = pick(table % PAR)
    sub = iota((128, 256), 0).astype(F32)
    mine = sub == owner
    at_row = onehot(sub == inrow)
    rank = mm(onehot(mine), onehot(iota((256, 256), 0) < iota((256, 256), 1)))
    lane = iota((256, 128), 1)
    high = jnp.floor(scnt[...] * (1.0 / 64.0))
    counts = jnp.where(lane == 64, high, jnp.where(lane == 65, scnt[...] - 64.0 * high, 0.0)).astype(BF16)
    sums = ssum[...].astype(BF16)
    for j in range(CAP):
        sel = onehot(mine & (rank == j))
        placed = mm(sel, sums)
        for c in range(3):
            x32[pl.ds(4 * j + c, DEVS, stride=MSG), :] = placed[:, c * 128:(c + 1) * 128]
        x32[pl.ds(4 * j + 3, DEVS, stride=MSG), :] = mm_nt(sel, at_row) + mm(sel, counts)
    for q in range(4 * CAP, MSG):
        x32[pl.ds(q, DEVS, stride=MSG), :] = jnp.zeros((DEVS, 128), F32)
    send[...] = x32[...].reshape(DEVS, MSG, 128).astype(BF16)

    def scatter(k, carry):
        o = lax.rem(me + k, DEVS)
        push(send.at[o], recv.at[me], 0, (o // N_SCENE, o % N_SCENE)).start()
        return carry

    lax.fori_loop(1, DEVS, scatter, 0)
    recv[me] = send[me]
    push(send.at[pl.ds(0, DEVS - 1)], recv.at[pl.ds(0, DEVS - 1)], 0, here).wait()

    x32[...] = recv[...].reshape(DEVS * MSG, 128).astype(F32)
    row = lambda q: x32[pl.ds(q, DEVS, stride=MSG), :].astype(BF16)
    picks = jnp.concatenate([row(4 * j + 3) for j in range(CAP)], axis=0)
    body = jnp.concatenate(
        [jnp.concatenate([row(4 * j + c) for c in range(4)], axis=1) for j in range(CAP)], axis=0
    )
    pooled = mm_t(picks, body)[:PAR]
    lane = iota((PAR, 128), 1)
    tail = pooled[:, 384:]
    count = jnp.sum(jnp.where(lane == 64, 64.0 * tail, jnp.where(lane == 65, tail, 0.0)), axis=-1, keepdims=True)
    for cp in loads[4:]:
        cp.wait()
    tokens = pooled[:, :384] / jnp.maximum(count, 1.0) + embed[...].astype(F32)
    attn_in = (layer_norm(tokens) * again_ref[...][None, :]).astype(BF16)
    ain[...] = attn_in
    aq[sp] = attn_in
    ak[sc] = attn_in

    def send_q(k, carry):
        push(ain, aq.at[sp], 1, (lax.rem(sp + k, N_SPACE), sc)).start()
        return carry

    def send_k(k, carry):
        push(ain, ak.at[sc], 2, (sp, lax.rem(sc + k, N_SCENE))).start()
        return carry

    lax.fori_loop(1, N_SPACE, send_q, 0)
    lax.fori_loop(1, N_SCENE, send_k, 0)
    push(aq.at[pl.ds(0, N_SPACE - 1)], aq.at[pl.ds(0, N_SPACE - 1)], 1, here).wait()
    qb[...] = (mm(aq[...].reshape(N_SPACE * PAR, 384), wqkv[:, :384]) * 0.125).astype(BF16)
    push(ak.at[pl.ds(0, N_SCENE - 1)], ak.at[pl.ds(0, N_SCENE - 1)], 2, here).wait()
    keys_in = ak[...].reshape(N_SCENE * PAR, 384)
    kb[...] = mm(keys_in, wqkv[:, 384:768]).astype(BF16)
    values = mm(keys_in, wqkv[:, 768:]).astype(BF16)
    for p in range(3):
        vb[:, p * 256:p * 256 + 128] = values[:, p * 128:(p + 1) * 128]
        vb[:, p * 256 + 128:(p + 1) * 256] = jnp.ones((N_SCENE * PAR, 128), BF16)

    rows = N_SPACE * PAR // 2
    lanes = iota((rows, 128), 1)
    for t in range(2):
        ts = pl.ds(t * rows, rows)
        stats = jnp.zeros((rows, 128), F32)
        for p in range(3):
            ps = pl.ds(p * 128, 128)
            q = qb[ts, ps]
            mixed = None
            for u in range(2):
                h = 2 * p + u
                scores = mm_nt(jnp.where((lanes >= 64) == (u == 1), q, jnp.zeros_like(q)), kb[:, ps])
                top = jnp.max(scores, axis=-1, keepdims=True)
                weights = jnp.exp(scores - top).astype(BF16)
                both = mm(weights, vb[:, p * 256:(p + 1) * 256])
                total = both[:, 128:]
                part = both[:, :128] / total
                mixed = part if u == 0 else jnp.where(lanes < 64, mixed, part)
                lse = top + jnp.log(total)
                s0 = lse.astype(BF16).astype(F32)
                s1 = (lse - s0).astype(BF16).astype(F32)
                s2 = lse - s0 - s1
                stats = jnp.where(lanes == h, s0, jnp.where(lanes == 8 + h, s1, jnp.where(lanes == 16 + h, s2, stats)))
            outb[pl.ds(t * 4, 4), :, ps] = mixed.astype(BF16).reshape(4, PAR, 128)
        outb[pl.ds(t * 4, 4), :, 384:] = stats.astype(BF16).reshape(4, PAR, 128)

    def send_o(k, carry):
        o = lax.rem(sp + k, N_SPACE)
        push(outb.at[o], inb.at[sp], 3, (o, sc)).start()
        return carry

    lax.fori_loop(1, N_SPACE, send_o, 0)
    inb[sp] = outb[sp]
    push(outb.at[pl.ds(0, N_SPACE - 1)], inb.at[pl.ds(0, N_SPACE - 1)], 3, here).wait()

    spread = onehot((iota((128, 384), 0) % 8 == iota((128, 384), 1) // 64) & (iota((128, 384), 0) < 24))
    lse = mm(inb[:, :, 384:].reshape(N_SPACE * PAR, 128), spread).reshape(N_SPACE, PAR, 384)
    share = jnp.exp(lse - jnp.max(lse, axis=0, keepdims=True))
    attended = jnp.sum(share * inb[:, :, :384].astype(F32), axis=0) / jnp.sum(share, axis=0)
    state = tokens + mm(attended.astype(BF16), wout[...])
    state_ref[...] = state.astype(BF16)
    class_in = layer_norm(state).astype(BF16)
    logits = mm_nt(wcls_ref[...], class_in)
    peak = jnp.max(logits, axis=0, keepdims=True)
    log_total = peak + jnp.log(jnp.sum(jnp.exp(logits - peak), axis=0, keepdims=True))
    picked = jnp.sum(jnp.where(iota(logits.shape, 0) == lab_ref[...], logits, 0.0), axis=0, keepdims=True)
    loss_ref[...] = log_total - picked

    def drain(k, carry):
        save(k).wait()
        return carry

    lax.fori_loop(0, 8, drain, 0)


def local(pixels, dw_kernel, dw_bias, norm_gain, w_expand, w_reduce, layer_scale, pixel_slot, intersection,
          parcel_pos, parcel_embed, attn_gain, w_qkv, w_out, w_class, labels):
    vmem = pl.BlockSpec(memory_space=pltpu.VMEM)
    hbm = pl.BlockSpec(memory_space=pl.ANY)
    dma = pltpu.SemaphoreType.DMA
    features, state, loss = pl.pallas_call(
        fused_kernel,
        out_shape=(
            jax.ShapeDtypeStruct((2, 16, 4, 16, 384), BF16),
            jax.ShapeDtypeStruct((PAR, 384), BF16),
            jax.ShapeDtypeStruct((1, PAR), F32),
        ),
        in_specs=[hbm] * 6 + [vmem] * 10,
        out_specs=(hbm, vmem, vmem),
        scratch_shapes=[
            pltpu.VMEM((2, 22, 4, 16, 384), BF16),
            pltpu.VMEM((49, 16, 384), BF16),
            pltpu.VMEM((4, 7, 4, 16, 384), BF16),
            pltpu.VMEM((256, 384), F32),
            pltpu.VMEM((2, 256, 384), BF16),
            pltpu.VMEM((8, 4, 4, 16, 384), BF16),
            pltpu.VMEM((256, 384), F32),
            pltpu.VMEM((256, 128), F32),
            pltpu.VMEM((64, 448), BF16),
            pltpu.VMEM((384, 1536), BF16),
            pltpu.VMEM((1536, 384), BF16),
            pltpu.VMEM((384, 1152), BF16),
            pltpu.VMEM((384, 384), BF16),
            pltpu.VMEM((PAR, 384), BF16),
            pltpu.VMEM((DEVS, MSG, 128), BF16),
            pltpu.VMEM((DEVS, MSG, 128), BF16),
            pltpu.VMEM((DEVS * MSG, 128), F32),
            pltpu.VMEM((PAR, 384), BF16),
            pltpu.VMEM((N_SPACE, PAR, 384), BF16),
            pltpu.VMEM((N_SCENE, PAR, 384), BF16),
            pltpu.VMEM((N_SPACE * PAR, 384), BF16),
            pltpu.VMEM((N_SCENE * PAR, 384), BF16),
            pltpu.VMEM((N_SCENE * PAR, 768), BF16),
            pltpu.VMEM((N_SPACE, PAR, 512), BF16),
            pltpu.VMEM((N_SPACE, PAR, 512), BF16),
            dma((7,)),
            dma((8,)),
            dma((6,)),
            dma((6,)),
        ],
        compiler_params=pltpu.CompilerParams(vmem_limit_bytes=63 << 20, collective_id=0, has_side_effects=True),
        name="fused",
    )(
        pixels.reshape(2, 16, 4, 16, 384), w_expand, w_reduce, w_qkv, w_out, parcel_embed, dw_kernel, dw_bias, norm_gain,
        layer_scale, pixel_slot, intersection, parcel_pos.reshape(64, 128), attn_gain, w_class.T, labels.reshape(1, PAR),
    )
    return features.reshape(2, 16, 64, 384), state, loss.reshape(PAR)


def solution(mesh):
    in_specs = (
        P("scene", "space", None, None), P(), P(), P(), P(), P(), P(), P("scene", "space", None),
        P(("space", "scene"), None), P(), P(("space", "scene"), None), P(), P(), P(), P(), P(("space", "scene")),
    )
    out_specs = (P("scene", "space", None, None), P(("space", "scene"), None), P(("space", "scene")))
    return jax.shard_map(local, mesh=mesh, in_specs=in_specs, out_specs=out_specs, check_vma=False)
```

```python
import jax
import jax.numpy as jnp
from jax import lax
from jax.experimental import pallas as pl
from jax.experimental.pallas import tpu as pltpu
from jax.sharding import PartitionSpec as P

EPS = 1e-06
N_SPACE = 8
N_SCENE = 16
DEVS = N_SPACE * N_SCENE
PAR = 64
CAP = 3
MSG = 16
F32 = jnp.float32
BF16 = jnp.bfloat16
MESH = pl.DeviceIdType.MESH
FLAT = pl.DeviceIdType.LOGICAL
GROUP = 8
HOPS = (
    (0, 0), (0, 1), (0, 3), (1, 0), (3, 0), (1, 1), (1, 3), (3, 1),
    (3, 3), (2, 0), (0, 2), (2, 1), (2, 3), (1, 2), (3, 2), (2, 2),
)


def mm(a, b):
    return jnp.dot(a, b, preferred_element_type=F32)


def mm_t(a, b):
    return lax.dot_general(a, b, (((0,), (0,)), ((), ())), preferred_element_type=F32)


def mm_nt(a, b):
    return lax.dot_general(a, b, (((1,), (1,)), ((), ())), preferred_element_type=F32)


def onehot(cond):
    return jnp.where(cond, 1.0, 0.0).astype(BF16)


def iota(shape, dim):
    return lax.broadcasted_iota(jnp.int32, shape, dim)


def layer_norm(x):
    centered = x - jnp.mean(x, axis=-1, keepdims=True)
    return centered * lax.rsqrt(jnp.mean(centered * centered, axis=-1, keepdims=True) + EPS)


def gelu(x):
    return 0.5 * x * (1.0 + lax.erf(x * 0.7071067811865476))


def fused_kernel(pix_hbm, w1_hbm, w2_hbm, wqkv_hbm, wout_hbm, embed_hbm, k_ref, bias_ref, gain_ref, ls_ref, slot_ref,
                 inter_ref, ppos_ref, again_ref, wcls_ref, lab_ref, feat_hbm, state_ref, loss_ref,
                 xs, taps, vs, sp32, nb, hid, fb, ssum, scnt, shm, w1, w2, wqkv, wout, embed, send, recv, x32, ain, aq, ak,
                 qb, tops, mixes, outb, inb, lsem, fsem, ssem, rsem, all_in):
    sp = lax.axis_index("space")
    sc = lax.axis_index("scene")
    me = sp * N_SCENE + sc
    here = (sp, sc)

    loads = [pltpu.make_async_copy(pix_hbm.at[s], xs.at[s, pl.ds(3, 16)], lsem.at[s]) for s in range(2)]
    pairs = ((w1_hbm, w1), (w2_hbm, w2), (wqkv_hbm, wqkv), (wout_hbm, wout), (embed_hbm, embed))
    loads += [pltpu.make_async_copy(a, b, lsem.at[2 + n]) for n, (a, b) in enumerate(pairs)]
    for cp in loads:
        cp.start()

    barrier = pltpu.get_barrier_semaphore()

    for k in range(1, N_SPACE):
        pl.semaphore_signal(barrier, inc=1, device_id=(lax.rem(sp + k, N_SPACE), sc), device_id_type=MESH)
    for k in range(1, N_SCENE):
        pl.semaphore_signal(barrier, inc=1, device_id=(sp, lax.rem(sc + k, N_SCENE)), device_id_type=MESH)

    def push(src, dst, n, dev):
        return pltpu.make_async_remote_copy(
            src_ref=src, dst_ref=dst, send_sem=ssem.at[n], recv_sem=rsem.at[n], device_id=dev, device_id_type=MESH
        )

    to_prev = push(xs.at[:, pl.ds(3, 3)], xs.at[:, pl.ds(19, 3)], 4, (lax.rem(sp + N_SPACE - 1, N_SPACE), sc))
    to_next = push(xs.at[:, pl.ds(16, 3)], xs.at[:, pl.ds(0, 3)], 5, (lax.rem(sp + 1, N_SPACE), sc))
    first, last = sp == 0, sp == N_SPACE - 1

    @pl.when(first)
    def _():
        xs[:, 0:3] = jnp.zeros((2, 3, 4, 16, 384), BF16)

    @pl.when(last)
    def _():
        xs[:, 19:22] = jnp.zeros((2, 3, 4, 16, 384), BF16)

    for a in range(7):
        k32 = k_ref[a].astype(F32)
        for b in range(7):
            taps[a * 7 + b] = jnp.broadcast_to(k32[b:b + 1, :], (16, 384)).astype(BF16)
    j = iota((64, 448), 1)
    shm[...] = onehot(j % 64 == iota((64, 448), 0) + j // 64 - 3)
    ssum[...] = jnp.zeros_like(ssum)
    scnt[...] = jnp.zeros_like(scnt)

    def place(k):
        inner = k < 4
        s = lax.rem(k, 4) // 2
        r0 = jnp.where(inner, 4 + 4 * lax.rem(k, 2), 12 * lax.rem(k, 2))
        return s, r0

    def conv(k):
        s, r0 = place(k)
        slot = lax.rem(k, 2)

        def piece(r, c):
            cs = pl.ds(c * 128, 128)
            acc = [None] * 7
            for a in range(7):
                x = xs[s, r0 + r + a, :, :, cs]
                for b in range(7):
                    p = x * taps[a * 7 + b, :, cs][None]
                    acc[b] = p if acc[b] is None else acc[b] + p
            for b in range(7):
                vs[r, b, :, :, cs] = acc[b]

        def row(r):
            sp32[pl.ds(r * 64, 64), :] = mm(shm[...], vs[r].reshape(448, 384)) + bias_ref[...][None, :]

        def norm():
            nb[slot] = (layer_norm(sp32[...]) * gain_ref[...][None, :]).astype(BF16)

        steps = []
        for r in range(4):
            steps += [lambda r=r, c=c: piece(r, c) for c in range(3)]
            steps.append(lambda r=r: row(r))
        return steps + [norm]

    def mlp(k):
        s, r0 = place(k)

        def part(h):
            hs = pl.ds(h * 512, 512)
            hid[:, hs] = gelu(mm(nb[lax.rem(k, 2)], w1[:, hs])).astype(BF16)

        def finish():
            cen = xs[s, pl.ds(r0 + 3, 4)].reshape(256, 384)
            f = (cen.astype(F32) + ls_ref[...][None, :] * mm(hid[...], w2[...])).astype(BF16)
            fb[k] = f.reshape(4, 4, 16, 384)
            save(k).start()
            slots = jnp.concatenate([slot_ref[s, pl.ds(r0 + r, 1), :] for r in range(4)], axis=1)
            m = onehot(iota((256, 256), 0) == slots)
            ssum[...] += mm(m, f)
            scnt[...] += mm(m, jnp.ones((256, 128), BF16))

        return [lambda h=h: part(h) for h in range(3)] + [finish]

    def save(k):
        s, r0 = place(k)
        return pltpu.make_async_copy(fb.at[k], feat_hbm.at[s, pl.ds(r0, 4)], fsem.at[k])

    def run(*lists):
        total = max(len(x) for x in lists)
        done = [0] * len(lists)
        for t in range(total):
            for n, x in enumerate(lists):
                while done[n] < len(x) and done[n] * total < (t + 1) * len(x):
                    x[done[n]]()
                    done[n] += 1

    loads[0].wait()
    loads[1].wait()
    run(conv(0))
    loads[2].wait()
    loads[3].wait()

    def stage(k, carry):
        @pl.when(k == 1)
        def _():
            pl.semaphore_wait(barrier, N_SPACE + N_SCENE - 2)
            for m in range(1, N_SCENE):
                pl.semaphore_signal(all_in, inc=1, device_id=(sp, lax.rem(sc + m, N_SCENE)), device_id_type=MESH)

            @pl.when(jnp.logical_not(first))
            def _():
                to_prev.start()

            @pl.when(jnp.logical_not(last))
            def _():
                to_next.start()

        @pl.when(k == 3)
        def _():
            @pl.when(jnp.logical_not(first))
            def _():
                to_prev.wait_send()
                to_next.wait_recv()

            @pl.when(jnp.logical_not(last))
            def _():
                to_next.wait_send()
                to_prev.wait_recv()

        run(mlp(k), conv(k + 1))
        return carry

    lax.fori_loop(0, 7, stage, 0)
    run(mlp(7))

    inter = inter_ref[...]
    hot = onehot(iota((64, 256), 0) == inter // 128)
    low = iota((128, 256), 0) == inter % 128
    table = ppos_ref[...]
    pick = lambda t: jnp.sum(jnp.where(low, mm_t(t.astype(F32).astype(BF16), hot), 0.0), axis=0, keepdims=True)
    owner = pick(table // PAR)
    inrow = pick(table % PAR)
    sub = iota((128, 256), 0).astype(F32)
    mine = sub == owner
    at_row = onehot(sub == inrow)
    rank = mm(onehot(mine), onehot(iota((256, 256), 0) < iota((256, 256), 1)))
    lane = iota((256, 128), 1)
    high = jnp.floor(scnt[...] * (1.0 / 64.0))
    counts = jnp.where(lane == 64, high, jnp.where(lane == 65, scnt[...] - 64.0 * high, 0.0)).astype(BF16)
    sums = ssum[...].astype(BF16)
    for j in range(CAP):
        sel = onehot(mine & (rank == j))
        placed = mm(sel, sums)
        for c in range(3):
            x32[pl.ds(4 * j + c, DEVS, stride=MSG), :] = placed[:, c * 128:(c + 1) * 128]
        x32[pl.ds(4 * j + 3, DEVS, stride=MSG), :] = mm_nt(sel, at_row) + mm(sel, counts)
    for q in range(4 * CAP, MSG):
        x32[pl.ds(q, DEVS, stride=MSG), :] = jnp.zeros((DEVS, 128), F32)
    send[...] = x32[...].reshape(DEVS, MSG, 128).astype(BF16)

    pl.semaphore_wait(all_in, N_SCENE - 1)
    z, core, x, y = sp // 2, lax.rem(sp, 2), sc // 4, lax.rem(sc, 4)
    space_at = [(lax.rem(z + d // 2, 4) * 2 + lax.rem(core + d % 2, 2)) * N_SCENE for d in range(N_SPACE)]
    scene_at = [lax.rem(x + d // 4, 4) * 4 + lax.rem(y + d % 4, 4) for d in range(N_SCENE)]
    ring = (0, 1, 2, 1)
    far = sorted(
        ((-ring[a // 2] - ring[b // 4] - ring[b % 4], a, b) for a in range(N_SPACE) for b in range(N_SCENE) if a + b > 0)
    )
    for _, a, b in far:
        o = space_at[a] + scene_at[b]
        pltpu.make_async_remote_copy(
            src_ref=send.at[o], dst_ref=recv.at[me], send_sem=ssem.at[0], recv_sem=rsem.at[0],
            device_id=o, device_id_type=FLAT,
        ).start()
    recv[me] = send[me]
    push(send.at[pl.ds(0, DEVS - 1)], recv.at[pl.ds(0, DEVS - 1)], 0, here).wait()

    x32[...] = recv[...].reshape(DEVS * MSG, 128).astype(F32)
    row = lambda q: x32[pl.ds(q, DEVS, stride=MSG), :].astype(BF16)
    picks = jnp.concatenate([row(4 * j + 3) for j in range(CAP)], axis=0)
    body = jnp.concatenate(
        [jnp.concatenate([row(4 * j + c) for c in range(4)], axis=1) for j in range(CAP)], axis=0
    )
    pooled = mm_t(picks, body)[:PAR]
    lane = iota((PAR, 128), 1)
    tail = pooled[:, 384:]
    count = jnp.sum(jnp.where(lane == 64, 64.0 * tail, jnp.where(lane == 65, tail, 0.0)), axis=-1, keepdims=True)
    for cp in loads[4:]:
        cp.wait()
    tokens = pooled[:, :384] / jnp.maximum(count, 1.0) + embed[...].astype(F32)
    attn_in = (layer_norm(tokens) * again_ref[...][None, :]).astype(BF16)
    ain[...] = attn_in
    aq[sp] = attn_in
    ak[0] = attn_in

    def send_q(k, carry):
        push(ain, aq.at[sp], 1, (lax.rem(sp + k, N_SPACE), sc)).start()
        return carry

    lax.fori_loop(1, N_SPACE, send_q, 0)
    groups = N_SCENE // GROUP
    for n in range(1, N_SCENE):
        dx, dy = HOPS[n]
        to = lax.rem(sc // 4 + dx, 4) * 4 + lax.rem(lax.rem(sc, 4) + dy, 4)
        push(ain, ak.at[n], 6 + n // GROUP, (sp, to)).start()
    push(aq.at[pl.ds(0, N_SPACE - 1)], aq.at[pl.ds(0, N_SPACE - 1)], 1, here).wait()
    qb[...] = (mm(aq[...].reshape(N_SPACE * PAR, 384), wqkv[:, :384]) * 0.125).astype(BF16)

    rows = N_SPACE * PAR // 2
    lanes = iota((rows, 128), 1)
    ones = jnp.ones((GROUP * PAR, 128), BF16)
    for g in range(groups):
        low = max(GROUP * g, 1)
        got = pl.ds(low, GROUP * (g + 1) - low)
        push(ak.at[got], ak.at[got], 6 + g, here).wait()
        keys_in = ak[pl.ds(GROUP * g, GROUP)].reshape(GROUP * PAR, 384)
        keys = mm(keys_in, wqkv[:, 384:768]).astype(BF16)
        values = mm(keys_in, wqkv[:, 768:]).astype(BF16)
        for t in range(2):
            ts = pl.ds(t * rows, rows)
            stats = jnp.zeros((rows, 128), F32)
            for p in range(3):
                ps = pl.ds(p * 128, 128)
                q = qb[ts, ps]
                wide = jnp.concatenate([values[:, p * 128:(p + 1) * 128], ones], axis=1)
                for u in range(2):
                    h = 2 * p + u
                    scores = mm_nt(
                        jnp.where((lanes >= 64) == (u == 1), q, jnp.zeros_like(q)), keys[:, p * 128:(p + 1) * 128]
                    )
                    top = jnp.max(scores, axis=-1, keepdims=True)
                    if g > 0:
                        before = tops[h, ts, :]
                        top = jnp.maximum(before[:, :1], top)
                    both = mm(jnp.exp(scores - top).astype(BF16), wide)
                    if g > 0:
                        fade = jnp.exp(before - top)
                        both = both + jnp.concatenate([fade, fade], axis=1) * mixes[h, ts, :]
                    if g < groups - 1:
                        tops[h, ts, :] = jnp.broadcast_to(top, (rows, 128))
                        mixes[h, ts, :] = both
                        continue
                    total = both[:, 128:]
                    part = both[:, :128] / total
                    mixed = part if u == 0 else jnp.where(lanes < 64, mixed, part)
                    lse = top + jnp.log(total)
                    s0 = lse.astype(BF16).astype(F32)
                    s1 = (lse - s0).astype(BF16).astype(F32)
                    s2 = lse - s0 - s1
                    stats = jnp.where(
                        lanes == h, s0, jnp.where(lanes == 8 + h, s1, jnp.where(lanes == 16 + h, s2, stats))
                    )
                if g == groups - 1:
                    outb[pl.ds(t * 4, 4), :, ps] = mixed.astype(BF16).reshape(4, PAR, 128)
            if g == groups - 1:
                outb[pl.ds(t * 4, 4), :, 384:] = stats.astype(BF16).reshape(4, PAR, 128)
                for o in range(4 * t, 4 * t + 4):
                    @pl.when(sp != o)
                    def _():
                        push(outb.at[o], inb.at[sp], 3, (o, sc)).start()

    inb[sp] = outb[sp]
    push(outb.at[pl.ds(0, N_SPACE - 1)], inb.at[pl.ds(0, N_SPACE - 1)], 3, here).wait()

    spread = onehot((iota((128, 384), 0) % 8 == iota((128, 384), 1) // 64) & (iota((128, 384), 0) < 24))
    lse = mm(inb[:, :, 384:].reshape(N_SPACE * PAR, 128), spread).reshape(N_SPACE, PAR, 384)
    share = jnp.exp(lse - jnp.max(lse, axis=0, keepdims=True))
    attended = jnp.sum(share * inb[:, :, :384].astype(F32), axis=0) / jnp.sum(share, axis=0)
    state = tokens + mm(attended.astype(BF16), wout[...])
    state_ref[...] = state.astype(BF16)
    class_in = layer_norm(state).astype(BF16)
    logits = mm_nt(wcls_ref[...], class_in)
    peak = jnp.max(logits, axis=0, keepdims=True)
    log_total = peak + jnp.log(jnp.sum(jnp.exp(logits - peak), axis=0, keepdims=True))
    picked = jnp.sum(jnp.where(iota(logits.shape, 0) == lab_ref[...], logits, 0.0), axis=0, keepdims=True)
    loss_ref[...] = log_total - picked

    def drain(k, carry):
        save(k).wait()
        return carry

    lax.fori_loop(0, 8, drain, 0)


def local(pixels, dw_kernel, dw_bias, norm_gain, w_expand, w_reduce, layer_scale, pixel_slot, intersection,
          parcel_pos, parcel_embed, attn_gain, w_qkv, w_out, w_class, labels):
    vmem = pl.BlockSpec(memory_space=pltpu.VMEM)
    hbm = pl.BlockSpec(memory_space=pl.ANY)
    dma = pltpu.SemaphoreType.DMA
    features, state, loss = pl.pallas_call(
        fused_kernel,
        out_shape=(
            jax.ShapeDtypeStruct((2, 16, 4, 16, 384), BF16),
            jax.ShapeDtypeStruct((PAR, 384), BF16),
            jax.ShapeDtypeStruct((1, PAR), F32),
        ),
        in_specs=[hbm] * 6 + [vmem] * 10,
        out_specs=(hbm, vmem, vmem),
        scratch_shapes=[
            pltpu.VMEM((2, 22, 4, 16, 384), BF16),
            pltpu.VMEM((49, 16, 384), BF16),
            pltpu.VMEM((4, 7, 4, 16, 384), BF16),
            pltpu.VMEM((256, 384), F32),
            pltpu.VMEM((2, 256, 384), BF16),
            pltpu.VMEM((256, 1536), BF16),
            pltpu.VMEM((8, 4, 4, 16, 384), BF16),
            pltpu.VMEM((256, 384), F32),
            pltpu.VMEM((256, 128), F32),
            pltpu.VMEM((64, 448), BF16),
            pltpu.VMEM((384, 1536), BF16),
            pltpu.VMEM((1536, 384), BF16),
            pltpu.VMEM((384, 1152), BF16),
            pltpu.VMEM((384, 384), BF16),
            pltpu.VMEM((PAR, 384), BF16),
            pltpu.VMEM((DEVS, MSG, 128), BF16),
            pltpu.VMEM((DEVS, MSG, 128), BF16),
            pltpu.VMEM((DEVS * MSG, 128), F32),
            pltpu.VMEM((PAR, 384), BF16),
            pltpu.VMEM((N_SPACE, PAR, 384), BF16),
            pltpu.VMEM((N_SCENE, PAR, 384), BF16),
            pltpu.VMEM((N_SPACE * PAR, 384), BF16),
            pltpu.VMEM((6, N_SPACE * PAR, 128), F32),
            pltpu.VMEM((6, N_SPACE * PAR, 256), F32),
            pltpu.VMEM((N_SPACE, PAR, 512), BF16),
            pltpu.VMEM((N_SPACE, PAR, 512), BF16),
            dma((7,)),
            dma((8,)),
            dma((10,)),
            dma((10,)),
            pltpu.SemaphoreType.REGULAR,
        ],
        compiler_params=pltpu.CompilerParams(vmem_limit_bytes=63 << 20, collective_id=0, has_side_effects=True),
        name="fused",
    )(
        pixels.reshape(2, 16, 4, 16, 384), w_expand, w_reduce, w_qkv, w_out, parcel_embed, dw_kernel, dw_bias, norm_gain,
        layer_scale, pixel_slot, intersection, parcel_pos.reshape(64, 128), attn_gain, w_class.T, labels.reshape(1, PAR),
    )
    return features.reshape(2, 16, 64, 384), state, loss.reshape(PAR)


def solution(mesh):
    in_specs = (
        P("scene", "space", None, None), P(), P(), P(), P(), P(), P(), P("scene", "space", None),
        P(("space", "scene"), None), P(), P(("space", "scene"), None), P(), P(), P(), P(), P(("space", "scene")),
    )
    out_specs = (P("scene", "space", None, None), P(("space", "scene"), None), P(("space", "scene")))
    return jax.shard_map(local, mesh=mesh, in_specs=in_specs, out_specs=out_specs, check_vma=False)
```

```python
import jax
import jax.numpy as jnp
from jax import lax
from jax.experimental import pallas as pl
from jax.experimental.pallas import tpu as pltpu
from jax.sharding import PartitionSpec as P

EPS = 1e-06
N_SPACE = 8
N_SCENE = 16
DEVS = N_SPACE * N_SCENE
PAR = 64
CAP = 3
MSG = 16
F32 = jnp.float32
BF16 = jnp.bfloat16
MESH = pl.DeviceIdType.MESH
FLAT = pl.DeviceIdType.LOGICAL
GROUPS = ((0, 12), (12, 16))
HOPS = (
    (0, 0), (0, 1), (0, 3), (1, 0), (3, 0), (1, 1), (1, 3), (3, 1),
    (3, 3), (2, 0), (0, 2), (2, 1), (2, 3), (1, 2), (3, 2), (2, 2),
)


def mm(a, b):
    return jnp.dot(a, b, preferred_element_type=F32)


def mm_t(a, b):
    return lax.dot_general(a, b, (((0,), (0,)), ((), ())), preferred_element_type=F32)


def mm_nt(a, b):
    return lax.dot_general(a, b, (((1,), (1,)), ((), ())), preferred_element_type=F32)


def onehot(cond):
    return jnp.where(cond, 1.0, 0.0).astype(BF16)


def iota(shape, dim):
    return lax.broadcasted_iota(jnp.int32, shape, dim)


def layer_norm(x):
    centered = x - jnp.mean(x, axis=-1, keepdims=True)
    return centered * lax.rsqrt(jnp.mean(centered * centered, axis=-1, keepdims=True) + EPS)


def gelu(x):
    return 0.5 * x * (1.0 + lax.erf(x * 0.7071067811865476))


def fused_kernel(pix_hbm, w1_hbm, w2_hbm, wqkv_hbm, wout_hbm, embed_hbm, k_ref, bias_ref, gain_ref, ls_ref, slot_ref,
                 inter_ref, ppos_ref, again_ref, wcls_ref, lab_ref, feat_hbm, state_ref, loss_ref,
                 xs, taps, vs, sp32, nb, hid, fb, ssum, scnt, shm, w1, w2, wqkv, wout, embed, send, recv, x32, ain, aq, ak,
                 qb, tops, mixes, outb, inb, lsem, fsem, ssem, rsem, all_in):
    sp = lax.axis_index("space")
    sc = lax.axis_index("scene")
    me = sp * N_SCENE + sc
    here = (sp, sc)

    loads = [pltpu.make_async_copy(pix_hbm.at[s], xs.at[s, pl.ds(3, 16)], lsem.at[s]) for s in range(2)]
    pairs = ((w1_hbm, w1), (w2_hbm, w2), (wqkv_hbm, wqkv), (wout_hbm, wout), (embed_hbm, embed))
    loads += [pltpu.make_async_copy(a, b, lsem.at[2 + n]) for n, (a, b) in enumerate(pairs)]
    for n in (0, 2, 3, 1, 4, 5, 6):
        loads[n].start()

    barrier = pltpu.get_barrier_semaphore()

    for k in range(1, N_SPACE):
        pl.semaphore_signal(barrier, inc=1, device_id=(lax.rem(sp + k, N_SPACE), sc), device_id_type=MESH)
    for k in range(1, N_SCENE):
        pl.semaphore_signal(barrier, inc=1, device_id=(sp, lax.rem(sc + k, N_SCENE)), device_id_type=MESH)

    def push(src, dst, n, dev):
        return pltpu.make_async_remote_copy(
            src_ref=src, dst_ref=dst, send_sem=ssem.at[n], recv_sem=rsem.at[n], device_id=dev, device_id_type=MESH
        )

    to_prev = push(xs.at[:, pl.ds(3, 3)], xs.at[:, pl.ds(19, 3)], 4, (lax.rem(sp + N_SPACE - 1, N_SPACE), sc))
    to_next = push(xs.at[:, pl.ds(16, 3)], xs.at[:, pl.ds(0, 3)], 5, (lax.rem(sp + 1, N_SPACE), sc))
    first, last = sp == 0, sp == N_SPACE - 1

    @pl.when(first)
    def _():
        xs[:, 0:3] = jnp.zeros((2, 3, 4, 16, 384), BF16)

    @pl.when(last)
    def _():
        xs[:, 19:22] = jnp.zeros((2, 3, 4, 16, 384), BF16)

    for a in range(7):
        k32 = k_ref[a].astype(F32)
        for b in range(7):
            taps[a * 7 + b] = jnp.broadcast_to(k32[b:b + 1, :], (16, 384)).astype(BF16)
    j = iota((64, 448), 1)
    shm[...] = onehot(j % 64 == iota((64, 448), 0) + j // 64 - 3)
    ssum[...] = jnp.zeros_like(ssum)
    scnt[...] = jnp.zeros_like(scnt)

    def place(k, half):
        return lax.rem(k, 2), jnp.where(k < 2, 4 + 4 * half, 12 * half)

    def conv(k):
        slot = lax.rem(k, 2)

        def piece(r, c):
            s, r0 = place(k, r // 4)
            cs = pl.ds(c * 128, 128)
            acc = [None] * 7
            for a in range(7):
                x = xs[s, r0 + r % 4 + a, :, :, cs]
                for b in range(7):
                    p = x * taps[a * 7 + b, :, cs][None]
                    acc[b] = p if acc[b] is None else acc[b] + p
            for b in range(7):
                vs[r % 4, b, :, :, cs] = acc[b]

        def row(r):
            sp32[pl.ds(r * 64, 64), :] = mm(shm[...], vs[r % 4].reshape(448, 384)) + bias_ref[...][None, :]

        def norm():
            nb[slot] = (layer_norm(sp32[...]) * gain_ref[...][None, :]).astype(BF16)

        steps = []
        for r in range(8):
            steps += [lambda r=r, c=c: piece(r, c) for c in range(3)]
            steps.append(lambda r=r: row(r))
        return steps + [norm]

    def mlp(k):
        def part(h):
            hs = pl.ds(h * 512, 512)
            hid[:, hs] = gelu(mm(nb[lax.rem(k, 2)], w1[:, hs])).astype(BF16)

        def finish():
            tail = mm(hid[...], w2[...])
            for half in range(2):
                s, r0 = place(k, half)
                cen = xs[s, pl.ds(r0 + 3, 4)].reshape(256, 384)
                f = (cen.astype(F32) + ls_ref[...][None, :] * tail[half * 256:(half + 1) * 256]).astype(BF16)
                fb[2 * k + half] = f.reshape(4, 4, 16, 384)
                save(k, half).start()
                slots = jnp.concatenate([slot_ref[s, pl.ds(r0 + r, 1), :] for r in range(4)], axis=1)
                m = onehot(iota((256, 256), 0) == slots)
                ssum[...] += mm(m, f)
                scnt[...] += mm(m, jnp.ones((256, 128), BF16))

        return [lambda h=h: part(h) for h in range(3)] + [finish]

    def save(k, half):
        s, r0 = place(k, half)
        return pltpu.make_async_copy(fb.at[2 * k + half], feat_hbm.at[s, pl.ds(r0, 4)], fsem.at[2 * k + half])

    def run(*lists):
        total = max(len(x) for x in lists)
        done = [0] * len(lists)
        for t in range(total):
            for n, x in enumerate(lists):
                while done[n] < len(x) and done[n] * total < (t + 1) * len(x):
                    x[done[n]]()
                    done[n] += 1

    loads[0].wait()
    run(conv(0))
    for cp in loads[1:4]:
        cp.wait()

    def stage(k, carry):
        @pl.when(k == 0)
        def _():
            pl.semaphore_wait(barrier, N_SPACE + N_SCENE - 2)
            for m in range(1, N_SCENE):
                pl.semaphore_signal(all_in, inc=1, device_id=(sp, lax.rem(sc + m, N_SCENE)), device_id_type=MESH)

            @pl.when(jnp.logical_not(first))
            def _():
                to_prev.start()

            @pl.when(jnp.logical_not(last))
            def _():
                to_next.start()

        @pl.when(k == 1)
        def _():
            @pl.when(jnp.logical_not(first))
            def _():
                to_prev.wait_send()
                to_next.wait_recv()

            @pl.when(jnp.logical_not(last))
            def _():
                to_next.wait_send()
                to_prev.wait_recv()

        run(mlp(k), conv(k + 1))
        return carry

    lax.fori_loop(0, 3, stage, 0)
    run(mlp(3))

    inter = inter_ref[...]
    hot = onehot(iota((64, 256), 0) == inter // 128)
    low = iota((128, 256), 0) == inter % 128
    table = ppos_ref[...]
    pick = lambda t: jnp.sum(jnp.where(low, mm_t(t.astype(F32).astype(BF16), hot), 0.0), axis=0, keepdims=True)
    owner = pick(table // PAR)
    inrow = pick(table % PAR)
    sub = iota((128, 256), 0).astype(F32)
    mine = sub == owner
    at_row = onehot(sub == inrow)
    rank = mm(onehot(mine), onehot(iota((256, 256), 0) < iota((256, 256), 1)))
    lane = iota((256, 128), 1)
    high = jnp.floor(scnt[...] * (1.0 / 64.0))
    counts = jnp.where(lane == 64, high, jnp.where(lane == 65, scnt[...] - 64.0 * high, 0.0)).astype(BF16)
    sums = ssum[...].astype(BF16)
    for j in range(CAP):
        sel = onehot(mine & (rank == j))
        placed = mm(sel, sums)
        for c in range(3):
            x32[pl.ds(4 * j + c, DEVS, stride=MSG), :] = placed[:, c * 128:(c + 1) * 128]
        x32[pl.ds(4 * j + 3, DEVS, stride=MSG), :] = mm_nt(sel, at_row) + mm(sel, counts)
    for q in range(4 * CAP, MSG):
        x32[pl.ds(q, DEVS, stride=MSG), :] = jnp.zeros((DEVS, 128), F32)
    send[...] = x32[...].reshape(DEVS, MSG, 128).astype(BF16)

    pl.semaphore_wait(all_in, N_SCENE - 1)
    z, core, x, y = sp // 2, lax.rem(sp, 2), sc // 4, lax.rem(sc, 4)
    space_at = [(lax.rem(z + d // 2, 4) * 2 + lax.rem(core + d % 2, 2)) * N_SCENE for d in range(N_SPACE)]
    scene_at = [lax.rem(x + d // 4, 4) * 4 + lax.rem(y + d % 4, 4) for d in range(N_SCENE)]
    ring = (0, 1, 2, 1)
    far = sorted(
        ((-ring[a // 2] - ring[b // 4] - ring[b % 4], a, b) for a in range(N_SPACE) for b in range(N_SCENE) if a + b > 0)
    )
    for _, a, b in far:
        o = space_at[a] + scene_at[b]
        pltpu.make_async_remote_copy(
            src_ref=send.at[o], dst_ref=recv.at[me], send_sem=ssem.at[0], recv_sem=rsem.at[0],
            device_id=o, device_id_type=FLAT,
        ).start()
    recv[me] = send[me]
    push(send.at[pl.ds(0, DEVS - 1)], recv.at[pl.ds(0, DEVS - 1)], 0, here).wait()

    x32[...] = recv[...].reshape(DEVS * MSG, 128).astype(F32)
    row = lambda q: x32[pl.ds(q, DEVS, stride=MSG), :].astype(BF16)
    picks = jnp.concatenate([row(4 * j + 3) for j in range(CAP)], axis=0)
    body = jnp.concatenate(
        [jnp.concatenate([row(4 * j + c) for c in range(4)], axis=1) for j in range(CAP)], axis=0
    )
    pooled = mm_t(picks, body)[:PAR]
    lane = iota((PAR, 128), 1)
    tail = pooled[:, 384:]
    count = jnp.sum(jnp.where(lane == 64, 64.0 * tail, jnp.where(lane == 65, tail, 0.0)), axis=-1, keepdims=True)
    for cp in loads[4:]:
        cp.wait()
    tokens = pooled[:, :384] / jnp.maximum(count, 1.0) + embed[...].astype(F32)
    attn_in = (layer_norm(tokens) * again_ref[...][None, :]).astype(BF16)
    ain[...] = attn_in
    aq[sp] = attn_in
    ak[0] = attn_in

    def send_q(k, carry):
        push(ain, aq.at[sp], 1, (lax.rem(sp + k, N_SPACE), sc)).start()
        return carry

    lax.fori_loop(1, N_SPACE, send_q, 0)
    groups = len(GROUPS)
    for n in range(1, N_SCENE):
        dx, dy = HOPS[n]
        to = lax.rem(sc // 4 + dx, 4) * 4 + lax.rem(lax.rem(sc, 4) + dy, 4)
        push(ain, ak.at[n], 6 + sum(n >= end for _, end in GROUPS), (sp, to)).start()
    push(aq.at[pl.ds(0, N_SPACE - 1)], aq.at[pl.ds(0, N_SPACE - 1)], 1, here).wait()
    qb[...] = (mm(aq[...].reshape(N_SPACE * PAR, 384), wqkv[:, :384]) * 0.125).astype(BF16)

    rows = N_SPACE * PAR // 2
    lanes = iota((rows, 128), 1)
    for g, (begin, end) in enumerate(GROUPS):
        ones = jnp.ones(((end - begin) * PAR, 128), BF16)
        low = max(begin, 1)
        got = pl.ds(low, end - low)
        push(ak.at[got], ak.at[got], 6 + g, here).wait()
        keys_in = ak[pl.ds(begin, end - begin)].reshape((end - begin) * PAR, 384)
        keys = mm(keys_in, wqkv[:, 384:768]).astype(BF16)
        values = mm(keys_in, wqkv[:, 768:]).astype(BF16)
        for t in range(2):
            ts = pl.ds(t * rows, rows)
            stats = jnp.zeros((rows, 128), F32)
            for p in range(3):
                ps = pl.ds(p * 128, 128)
                q = qb[ts, ps]
                wide = jnp.concatenate([values[:, p * 128:(p + 1) * 128], ones], axis=1)
                for u in range(2):
                    h = 2 * p + u
                    scores = mm_nt(
                        jnp.where((lanes >= 64) == (u == 1), q, jnp.zeros_like(q)), keys[:, p * 128:(p + 1) * 128]
                    )
                    top = jnp.max(scores, axis=-1, keepdims=True)
                    if g > 0:
                        before = tops[h, ts, :]
                        top = jnp.maximum(before[:, :1], top)
                    both = mm(jnp.exp(scores - top).astype(BF16), wide)
                    if g > 0:
                        fade = jnp.exp(before - top)
                        both = both + jnp.concatenate([fade, fade], axis=1) * mixes[h, ts, :]
                    if g < groups - 1:
                        tops[h, ts, :] = jnp.broadcast_to(top, (rows, 128))
                        mixes[h, ts, :] = both
                        continue
                    total = both[:, 128:]
                    part = both[:, :128] / total
                    mixed = part if u == 0 else jnp.where(lanes < 64, mixed, part)
                    lse = top + jnp.log(total)
                    s0 = lse.astype(BF16).astype(F32)
                    s1 = (lse - s0).astype(BF16).astype(F32)
                    s2 = lse - s0 - s1
                    stats = jnp.where(
                        lanes == h, s0, jnp.where(lanes == 8 + h, s1, jnp.where(lanes == 16 + h, s2, stats))
                    )
                if g == groups - 1:
                    outb[pl.ds(t * 4, 4), :, ps] = mixed.astype(BF16).reshape(4, PAR, 128)
            if g == groups - 1:
                outb[pl.ds(t * 4, 4), :, 384:] = stats.astype(BF16).reshape(4, PAR, 128)
                for o in range(4 * t, 4 * t + 4):
                    @pl.when(sp != o)
                    def _():
                        push(outb.at[o], inb.at[sp], 3, (o, sc)).start()

    inb[sp] = outb[sp]
    push(outb.at[pl.ds(0, N_SPACE - 1)], inb.at[pl.ds(0, N_SPACE - 1)], 3, here).wait()

    spread = onehot((iota((128, 384), 0) % 8 == iota((128, 384), 1) // 64) & (iota((128, 384), 0) < 24))
    lse = mm(inb[:, :, 384:].reshape(N_SPACE * PAR, 128), spread).reshape(N_SPACE, PAR, 384)
    share = jnp.exp(lse - jnp.max(lse, axis=0, keepdims=True))
    attended = jnp.sum(share * inb[:, :, :384].astype(F32), axis=0) / jnp.sum(share, axis=0)
    state = tokens + mm(attended.astype(BF16), wout[...])
    state_ref[...] = state.astype(BF16)
    class_in = layer_norm(state).astype(BF16)
    logits = mm_nt(wcls_ref[...], class_in)
    peak = jnp.max(logits, axis=0, keepdims=True)
    log_total = peak + jnp.log(jnp.sum(jnp.exp(logits - peak), axis=0, keepdims=True))
    picked = jnp.sum(jnp.where(iota(logits.shape, 0) == lab_ref[...], logits, 0.0), axis=0, keepdims=True)
    loss_ref[...] = log_total - picked

    def drain(k, carry):
        save(k, 0).wait()
        save(k, 1).wait()
        return carry

    lax.fori_loop(0, 4, drain, 0)


def local(pixels, dw_kernel, dw_bias, norm_gain, w_expand, w_reduce, layer_scale, pixel_slot, intersection,
          parcel_pos, parcel_embed, attn_gain, w_qkv, w_out, w_class, labels):
    vmem = pl.BlockSpec(memory_space=pltpu.VMEM)
    hbm = pl.BlockSpec(memory_space=pl.ANY)
    dma = pltpu.SemaphoreType.DMA
    features, state, loss = pl.pallas_call(
        fused_kernel,
        out_shape=(
            jax.ShapeDtypeStruct((2, 16, 4, 16, 384), BF16),
            jax.ShapeDtypeStruct((PAR, 384), BF16),
            jax.ShapeDtypeStruct((1, PAR), F32),
        ),
        in_specs=[hbm] * 6 + [vmem] * 10,
        out_specs=(hbm, vmem, vmem),
        scratch_shapes=[
            pltpu.VMEM((2, 22, 4, 16, 384), BF16),
            pltpu.VMEM((49, 16, 384), BF16),
            pltpu.VMEM((4, 7, 4, 16, 384), BF16),
            pltpu.VMEM((512, 384), F32),
            pltpu.VMEM((2, 512, 384), BF16),
            pltpu.VMEM((512, 1536), BF16),
            pltpu.VMEM((8, 4, 4, 16, 384), BF16),
            pltpu.VMEM((256, 384), F32),
            pltpu.VMEM((256, 128), F32),
            pltpu.VMEM((64, 448), BF16),
            pltpu.VMEM((384, 1536), BF16),
            pltpu.VMEM((1536, 384), BF16),
            pltpu.VMEM((384, 1152), BF16),
            pltpu.VMEM((384, 384), BF16),
            pltpu.VMEM((PAR, 384), BF16),
            pltpu.VMEM((DEVS, MSG, 128), BF16),
            pltpu.VMEM((DEVS, MSG, 128), BF16),
            pltpu.VMEM((DEVS * MSG, 128), F32),
            pltpu.VMEM((PAR, 384), BF16),
            pltpu.VMEM((N_SPACE, PAR, 384), BF16),
            pltpu.VMEM((N_SCENE, PAR, 384), BF16),
            pltpu.VMEM((N_SPACE * PAR, 384), BF16),
            pltpu.VMEM((6, N_SPACE * PAR, 128), F32),
            pltpu.VMEM((6, N_SPACE * PAR, 256), F32),
            pltpu.VMEM((N_SPACE, PAR, 512), BF16),
            pltpu.VMEM((N_SPACE, PAR, 512), BF16),
            dma((7,)),
            dma((8,)),
            dma((10,)),
            dma((10,)),
            pltpu.SemaphoreType.REGULAR,
        ],
        compiler_params=pltpu.CompilerParams(vmem_limit_bytes=63 << 20, collective_id=0, has_side_effects=True),
        name="fused",
    )(
        pixels.reshape(2, 16, 4, 16, 384), w_expand, w_reduce, w_qkv, w_out, parcel_embed, dw_kernel, dw_bias, norm_gain,
        layer_scale, pixel_slot, intersection, parcel_pos.reshape(64, 128), attn_gain, w_class.T, labels.reshape(1, PAR),
    )
    return features.reshape(2, 16, 64, 384), state, loss.reshape(PAR)


def solution(mesh):
    in_specs = (
        P("scene", "space", None, None), P(), P(), P(), P(), P(), P(), P("scene", "space", None),
        P(("space", "scene"), None), P(), P(("space", "scene"), None), P(), P(), P(), P(), P(("space", "scene")),
    )
    out_specs = (P("scene", "space", None, None), P(("space", "scene"), None), P(("space", "scene")))
    return jax.shard_map(local, mesh=mesh, in_specs=in_specs, out_specs=out_specs, check_vma=False)
```
